32 devices in a mesh: dp: 2 (over x), ctx: 16 (over z, y, core).
Axes of the slice: x: 2, y: 2, z: 4, core: 2. Of those that a mesh axis runs over, the one named last changes fastest.
Arguments:
- queries: bfloat16 [2, 6144, 4096], P('dp', 'ctx'), may hold values from -6 to 6
- keys: bfloat16 [2, 6144, 4096], P('dp', 'ctx'), may hold values from -6 to 6
- values: bfloat16 [2, 6144, 4096], P('dp', 'ctx'), may hold values from -6 to 6
- out_grad: bfloat16 [2, 6144, 4096], P('dp', 'ctx'), may hold values from -15 to 15
- gain: float32 [4096], replicated, may hold values from 0.1 to 1.9
Outputs:
- output: bfloat16 [2, 6144, 4096], P('dp', 'ctx')
- grad_queries: bfloat16 [2, 6144, 4096], P('dp', 'ctx')
- grad_keys: bfloat16 [2, 6144, 4096], P('dp', 'ctx')
- grad_values: bfloat16 [2, 6144, 4096], P('dp', 'ctx')
- grad_gain: float32 [4096], replicated
The draws below stay inside these ranges and needn't reach their ends.
All inputs are finite; a program needn't handle non-finite values.
Results may differ from the reference program's by a relative error of at most 0.007.
Values sent between devices are 32-bit elements; how exact they have to be, the bound alone decides.
A program may use at most 256 MiB of HBM per device.

```python
import jax
import jax.numpy as jnp
from jax import lax

HEADS = 32
HD = 128
TOK_DEV = 384
TOKENS = 6144
SEQS = 2
N_CTX = 16


def draw_out_grad(key, part):
    position = jnp.arange(TOKENS, dtype=jnp.float32) / TOKENS
    scaling = (1.0 + 2.0 * position)[None, :, None]
    result = jnp.clip(jax.random.normal(key, (SEQS, TOKENS, HEADS * HD), jnp.float32), -5.0, 5.0) * scaling
    return result.astype(jnp.bfloat16)


def level_of(own_key, extent, cuts, least, top_value):
    def one(dim, shards_of):
        heights = jax.random.uniform(jax.random.fold_in(jax.random.fold_in(own_key, 6), dim), (shards_of,), jnp.float32, least / len(cuts), top_value / len(cuts))
        return jnp.repeat(jnp.exp(heights), extent[dim] // shards_of).reshape((-1,) + (1,) * (len(extent) - dim - 1))

    loudness = one(*cuts[0])
    for cut in cuts[1:]:
        loudness = loudness * one(*cut)
    return loudness


def scatter_about(rng, dims, scale, most, pieces=(), kind=jnp.bfloat16):
    array = scale * jax.random.normal(rng, dims, jnp.float32)
    if pieces:
        array = array * level_of(rng, dims, pieces, -0.22, 0.18)
    return jnp.clip(array, -most, most).astype(kind)


def setup_inputs(seed: int = 0) -> dict:
    seeds = jax.random.split(jax.random.key(seed), 6)
    return {
        "queries": scatter_about(seeds[0], (SEQS, TOKENS, HEADS * HD), 1.0, 6.0, ((0, 2), (1, 16))),
        "keys": scatter_about(seeds[1], (SEQS, TOKENS, HEADS * HD), 1.0, 6.0, ((0, 2), (1, 16))),
        "values": scatter_about(seeds[2], (SEQS, TOKENS, HEADS * HD), 1.0, 6.0, ((0, 2), (1, 16))),
        "out_grad": draw_out_grad(jax.random.fold_in(seeds[5], 71), 0),
        "gain": jnp.clip(1.0 + 0.18 * jax.random.normal(seeds[4], (HEADS * HD,), jnp.float32), 0.1, 1.9),
    }


EPS = 1e-06
HIGH = lax.Precision.HIGHEST

def causal_mask(length):
    row_index = lax.broadcasted_iota(jnp.int32, (length, length), 0)
    col_index = lax.broadcasted_iota(jnp.int32, (length, length), 1)
    return row_index >= col_index

def score_block(query, key_rows):
    scores = jnp.einsum('ihd,jhd->hij', query.astype(jnp.float32), key_rows.astype(jnp.float32), precision=HIGH)
    return jnp.where(causal_mask(query.shape[0])[None], scores, 0.0).astype(jnp.bfloat16)

def forward_block(items):
    query, key_rows, value, grad_out, prefix_bf, gain_rows = items
    scores = score_block(query, key_rows)
    attended = jnp.einsum('hij,jhe->ihe', scores.astype(jnp.float32), value.astype(jnp.float32), precision=HIGH)
    attended = attended + jnp.einsum('ihd,hde->ihe', query.astype(jnp.float32), prefix_bf.astype(jnp.float32), precision=HIGH)
    inverse = lax.rsqrt(lax.optimization_barrier(jnp.mean(attended * attended, axis=-1, keepdims=True)) + EPS)
    normed = attended * inverse
    output = (normed * gain_rows).astype(jnp.bfloat16)
    grad_float = grad_out.astype(jnp.float32)
    gain_term = lax.optimization_barrier(jnp.sum(grad_float * normed, axis=0))
    scaled = grad_float * gain_rows
    dattn = (inverse * (scaled - normed * lax.optimization_barrier(jnp.mean(scaled * normed, axis=-1, keepdims=True)))).astype(jnp.bfloat16)
    gstate = jnp.einsum('ihd,ihe->hde', query.astype(jnp.float32), dattn.astype(jnp.float32), precision=HIGH)
    return (output, dattn, gain_term, gstate)

def backward_block(items):
    query, key_rows, value, dattn, prefix_bf, suffix_bf = items
    query_f = query.astype(jnp.float32)
    key_f = key_rows.astype(jnp.float32)
    value_f = value.astype(jnp.float32)
    dattn_f = dattn.astype(jnp.float32)
    scores = score_block(query, key_rows).astype(jnp.float32)
    dscore = jnp.einsum('ihe,jhe->hij', dattn_f, value_f, precision=HIGH)
    dscore = jnp.where(causal_mask(query.shape[0])[None], dscore, 0.0).astype(jnp.bfloat16).astype(jnp.float32)
    prefix_f = prefix_bf.astype(jnp.float32)
    suffix_f = suffix_bf.astype(jnp.float32)
    grad_q = jnp.einsum('hij,jhd->ihd', dscore, key_f, precision=HIGH) + jnp.einsum('ihe,hde->ihd', dattn_f, prefix_f, precision=HIGH)
    grad_k = jnp.einsum('hij,ihd->jhd', dscore, query_f, precision=HIGH) + jnp.einsum('jhe,hde->jhd', value_f, suffix_f, precision=HIGH)
    grad_v = jnp.einsum('hij,ihe->jhe', scores, dattn_f, precision=HIGH) + jnp.einsum('jhd,hde->jhe', key_f, suffix_f, precision=HIGH)
    return (grad_q.astype(jnp.bfloat16), grad_k.astype(jnp.bfloat16), grad_v.astype(jnp.bfloat16))

def reference(queries, keys, values, out_grad, gain):
    gain_rows = gain.reshape(HEADS, HD)
    shape4 = (N_CTX, TOK_DEV, HEADS, HD)
    outputs, grads_q, grads_k, grads_v = ([], [], [], [])
    grad_gain = jnp.zeros((HEADS, HD), jnp.float32)
    for seq in range(SEQS):
        query = queries[seq].reshape(shape4)
        key_rows = keys[seq].reshape(shape4)
        value = values[seq].reshape(shape4)
        grad_out = out_grad[seq].reshape(shape4)
        states = jnp.einsum('bjhd,bjhe->bhde', key_rows.astype(jnp.float32), value.astype(jnp.float32), precision=HIGH)
        zeros = jnp.zeros((1, HEADS, HD, HD), jnp.float32)
        prefix = jnp.concatenate([zeros, jnp.cumsum(states, axis=0)[:-1]], axis=0).astype(jnp.bfloat16)
        gain_many = jnp.broadcast_to(gain_rows, (N_CTX, HEADS, HD))
        output, dattn, gain_terms, gstates = lax.map(forward_block, (query, key_rows, value, grad_out, prefix, gain_many))
        grad_gain = grad_gain + lax.optimization_barrier(jnp.sum(gain_terms, axis=0))
        inclusive = jnp.cumsum(gstates[::-1], axis=0)[::-1]
        suffix = jnp.concatenate([inclusive[1:], zeros], axis=0).astype(jnp.bfloat16)
        grad_q, grad_k, grad_v = lax.map(backward_block, (query, key_rows, value, dattn, prefix, suffix))
        outputs.append(output.reshape(TOKENS, HEADS * HD))
        grads_q.append(grad_q.reshape(TOKENS, HEADS * HD))
        grads_k.append(grad_k.reshape(TOKENS, HEADS * HD))
        grads_v.append(grad_v.reshape(TOKENS, HEADS * HD))
    return (jnp.stack(outputs), jnp.stack(grads_q), jnp.stack(grads_k), jnp.stack(grads_v), grad_gain.reshape(HEADS * HD))
```

```python
import functools

import jax
import jax.numpy as jnp
from jax import lax
from jax.experimental import pallas as pl
from jax.experimental.pallas import tpu as pltpu
from jax.sharding import PartitionSpec as P

HD = 128
PW = 2 * HD
EPS = 1e-06
F32 = jnp.float32
BF16 = jnp.bfloat16
MESH = pl.DeviceIdType.MESH

LAG_FWD = 2
LAG_GY = 4
LAG_GZ = 6
LAG_STEP = 4
LAG_FIN = 2
LAG_PRO = 3
LAG_TURN = 4


def nt(a, b):
    return lax.dot_general(a, b, (((1,), (1,)), ((), ())), preferred_element_type=F32)


def nn(a, b):
    return lax.dot_general(a, b, (((1,), (0,)), ((), ())), preferred_element_type=F32)


def tn(a, b):
    return lax.dot_general(a, b, (((0,), (0,)), ((), ())), preferred_element_type=F32)


def kernel(
    ndp, nctx, pairs,
    q_hbm, k_hbm, v_hbm, g_hbm, gain_ref,
    gb, qb, kb, vb, gg_ref,
    kept, held,
    s_all, x_in, c_out, y_in, e_in, e_out, p_out, p_all,
    t_all, tx_in, tc_out, ty_in, te_in, te_out, tp_out, tp_all,
    gsum, grecv,
    io_sem, send_sem, recv_sem, gs_sem, gr_sem,
):
    dp = lax.axis_index("dp")
    me = lax.axis_index("ctx")
    c = lax.rem(me, 2)
    y = lax.rem(me // 2, 2)
    z = me // 4
    nz = nctx // 4
    sib = (dp, me + 1 - 2 * c)
    ypeer = (dp, me + 2 - 4 * y)
    up = (dp, lax.min(me + 4, nctx - 1))
    down = (dp, lax.max(me - 4, 0))
    length = qb.shape[1]

    steps = []
    bit = 1
    while bit < ndp:
        steps.append((dp + bit - 2 * bit * lax.rem(dp // bit, 2), me))
        bit *= 2
    n_dp = len(steps)
    bit = 1
    while bit < nctx:
        steps.append((dp, me + bit - 2 * bit * lax.rem(me // bit, 2)))
        bit *= 2

    def loads(p):
        cols = pl.ds(pl.multiple_of(p * PW, PW), PW)
        return [
            pltpu.make_async_copy(h.at[0, :, cols], b.at[p], io_sem.at[i, p])
            for i, (h, b) in enumerate(((k_hbm, kb), (v_hbm, vb), (q_hbm, qb), (g_hbm, gb)))
        ]

    def hop(kind, src, dst, p, to):
        return pltpu.make_async_remote_copy(
            src_ref=src, dst_ref=dst, send_sem=send_sem.at[kind], recv_sem=recv_sem.at[kind, p],
            device_id=to, device_id_type=MESH,
        )

    def load_kv(p, _):
        for copy in loads(p)[:2]:
            copy.start()
        return 0

    def load_qg(p, _):
        for copy in loads(p)[2:]:
            copy.start()
        return 0

    lax.fori_loop(0, pairs, load_kv, 0)
    lax.fori_loop(0, pairs, load_qg, 0)

    barrier = pltpu.get_barrier_semaphore()
    greet = [sib, ypeer] + steps[:n_dp] + steps[n_dp + 3:]
    for other in greet:
        pl.semaphore_signal(barrier, inc=1, device_id=other, device_id_type=MESH)

    @pl.when(z < nz - 1)
    def _():
        pl.semaphore_signal(barrier, inc=1, device_id=up, device_id_type=MESH)

    @pl.when(z > 0)
    def _():
        pl.semaphore_signal(barrier, inc=1, device_id=down, device_id_type=MESH)

    expected = len(greet) + lax.min(z, 1) + lax.min(nz - 1 - z, 1)
    pl.semaphore_wait(barrier, expected)

    @pl.when(z == 0)
    def _():
        e_in[...] = jnp.zeros_like(e_in)

    @pl.when(z == nz - 1)
    def _():
        te_in[...] = jnp.zeros_like(te_in)

    def to_chip(p, kind, all_ref, in_ref):
        return hop(kind, all_ref.at[1 - c, p], in_ref.at[p], p, sib)

    def chip_total(p, kind, all_ref, in_ref, out_ref, y_ref):
        to_chip(p, kind, all_ref, in_ref).wait_recv()
        out_ref[p] = all_ref[c, p] + in_ref[p]
        hop(kind + 1, out_ref.at[p], y_ref.at[p], p, ypeer).start()

    def along(p, kind, all_ref, in_ref, out_ref, y_ref, e_ref, eo_ref, po_ref, pa_ref, reverse):
        first = nz - 1 if reverse else 0
        last = nz - 1 - first
        to = down if reverse else up
        hop(kind + 1, out_ref.at[p], y_ref.at[p], p, ypeer).wait_recv()

        @pl.when(z != first)
        def _():
            hop(kind + 2, eo_ref.at[p], e_ref.at[p], p, to).wait_recv()

        entering = e_ref[p]
        across = y_ref[p]

        @pl.when(z != last)
        def _():
            eo_ref[p] = entering + (out_ref[p] + across)
            hop(kind + 2, eo_ref.at[p], e_ref.at[p], p, to).start()

        has_y = (y == 0) if reverse else (y == 1)
        mine_later = (c == 0) if reverse else (c == 1)
        base = entering + jnp.where(has_y, across, 0.0)
        po_ref[p] = base + jnp.where(mine_later, 0.0, all_ref[c, p])
        hop(kind + 3, po_ref.at[p], pa_ref.at[c, p], p, sib).start()
        pa_ref[c, p] = base + jnp.where(mine_later, in_ref[p], 0.0)

    fwd = (0, s_all, x_in, c_out, y_in)
    bwd = (4, t_all, tx_in, tc_out, ty_in)

    def prologue(t, _):
        @pl.when(t < pairs)
        def _():
            for copy in loads(t)[:2]:
                copy.wait()
            for j in range(2):
                at = slice(j * HD, (j + 1) * HD)
                s_all[j, t] = tn(kb[t, :, at], vb[t, :, at])
            to_chip(t, 0, s_all, x_in).start()

        @pl.when(t >= LAG_PRO)
        def _():
            chip_total(t - LAG_PRO, *fwd)
        return 0

    lax.fori_loop(0, pairs + LAG_PRO, prologue, 0)

    def forward(p):
        for copy in loads(p)[2:]:
            copy.wait()
        hop(3, p_out.at[p], p_all.at[1 - c, p], p, sib).wait_recv()
        row = lax.broadcasted_iota(jnp.int32, (length, length), 0)
        col = lax.broadcasted_iota(jnp.int32, (length, length), 1)
        causal = row >= col
        two = range(2)
        at = [slice(j * HD, (j + 1) * HD) for j in two]
        lanes = [pl.ds(pl.multiple_of(p * PW + j * HD, HD), HD) for j in two]
        query = [qb[p, :, at[j]] for j in two]
        key_rows = [kb[p, :, at[j]] for j in two]
        value = [vb[p, :, at[j]] for j in two]
        grad = [gb[p, :, at[j]].astype(F32) for j in two]
        prefix = [p_all[j, p].astype(BF16) for j in two]
        gain = [gain_ref[:, lanes[j]] for j in two]
        scores = [jnp.where(causal, nt(query[j], key_rows[j]), 0.0).astype(BF16) for j in two]
        attended = [
            nn(
                jnp.concatenate([scores[j], query[j]], axis=1),
                jnp.concatenate([value[j], prefix[j]], axis=0),
            )
            for j in two
        ]
        inverse = [
            lax.rsqrt(jnp.mean(attended[j] * attended[j], axis=-1, keepdims=True) + EPS) for j in two
        ]
        normed = [attended[j] * inverse[j] for j in two]
        product = [grad[j] * normed[j] for j in two]
        mean = [jnp.mean(product[j] * gain[j], axis=-1, keepdims=True) for j in two]
        dattn = [
            (inverse[j] * (grad[j] * gain[j] - normed[j] * mean[j])).astype(BF16) for j in two
        ]
        gstate = [tn(query[j], dattn[j]) for j in two]
        for j in two:
            t_all[j, p] = gstate[j]
        to_chip(p, 4, t_all, tx_in).start()
        for j in two:
            kept[p, :, at[j]] = dattn[j]
            held[j, p] = scores[j]
            gsum[0, :, lanes[j]] = jnp.sum(product[j], axis=0, keepdims=True)
            gb[p, :, at[j]] = (normed[j] * gain[j]).astype(BF16)

    def final(p):
        hop(7, tp_out.at[p], tp_all.at[1 - c, p], p, sib).wait_recv()
        row = lax.broadcasted_iota(jnp.int32, (length, length), 0)
        col = lax.broadcasted_iota(jnp.int32, (length, length), 1)
        causal = row >= col
        two = range(2)
        at = [slice(j * HD, (j + 1) * HD) for j in two]
        query = [qb[p, :, at[j]] for j in two]
        key_rows = [kb[p, :, at[j]] for j in two]
        value = [vb[p, :, at[j]] for j in two]
        dattn = [kept[p, :, at[j]] for j in two]
        prefix = [p_all[j, p].astype(BF16) for j in two]
        suffix = [tp_all[j, p].astype(BF16) for j in two]
        dscore = [jnp.where(causal, nt(dattn[j], value[j]), 0.0).astype(BF16) for j in two]
        grad_v = [
            (tn(held[j, p], dattn[j]) + nn(key_rows[j], suffix[j])).astype(BF16) for j in two
        ]
        grad_q = [
            nn(
                jnp.concatenate([dscore[j], dattn[j]], axis=1),
                jnp.concatenate([key_rows[j], prefix[j].T], axis=0),
            ).astype(BF16)
            for j in two
        ]
        grad_k = [
            (tn(dscore[j], query[j]) + nt(value[j], suffix[j])).astype(BF16) for j in two
        ]
        for j in two:
            qb[p, :, at[j]] = grad_q[j]
            kb[p, :, at[j]] = grad_k[j]
            vb[p, :, at[j]] = grad_v[j]

    def gain_hop(i):
        return pltpu.make_async_remote_copy(
            src_ref=gsum.at[i], dst_ref=grecv.at[i], send_sem=gs_sem.at[i], recv_sem=gr_sem.at[i],
            device_id=steps[i], device_id_type=MESH,
        )

    lag_gz = LAG_GZ + LAG_STEP * (nz - 1 - z)
    after = pairs + LAG_FWD
    lag_fin = lax.max(lag_gz + LAG_FIN, after + LAG_TURN * (z // (nz - 1)))
    gain_at = after
    total = max(
        pairs + max(LAG_GZ + LAG_STEP * (nz - 1) + LAG_FIN, after + LAG_TURN),
        gain_at + 2 * len(steps) + 1,
    )

    def guarded(p, stage):
        @pl.when(jnp.logical_and(p >= 0, p < pairs))
        def _():
            stage(p)

    def main(t, _):
        guarded(t, lambda p: along(p, *fwd, e_in, e_out, p_out, p_all, False))
        guarded(t - LAG_FWD, forward)
        guarded(t - LAG_GY, lambda p: chip_total(p, *bwd))
        guarded(t - lag_gz, lambda p: along(p, *bwd, te_in, te_out, tp_out, tp_all, True))
        guarded(t - lag_fin, final)
        for i in range(len(steps) + 1):
            @pl.when(t == gain_at + 2 * i)
            def _():
                if i > 0:
                    gain_hop(i - 1).wait_recv()
                    gsum[i] = gsum[i - 1] + grecv[i - 1]
                if i < len(steps):
                    gain_hop(i).start()
        return 0

    lax.fori_loop(0, total, main, 0)
    gg_ref[...] = gsum[len(steps)]

    for i in range(len(steps)):
        gain_hop(i).wait_send()
    for kind, all_ref, in_ref, out_ref, y_ref, eo_ref, e_ref, po_ref, pa_ref in (
        (*fwd, e_out, e_in, p_out, p_all),
        (*bwd, te_out, te_in, tp_out, tp_all),
    ):
        hop(kind, all_ref.at[1 - c], in_ref, 0, sib).wait_send()
        hop(kind + 1, out_ref, y_ref, 0, ypeer).wait_send()
        reverse = kind == 4

        @pl.when(z != (0 if reverse else nz - 1))
        def _():
            hop(kind + 2, eo_ref, e_ref, 0, down if reverse else up).wait_send()

        hop(kind + 3, po_ref, pa_ref.at[c], 0, sib).wait_send()


def settle(pairs, *refs):
    sources, total, targets, result, sems = refs[:4], refs[4], refs[5:9], refs[9], refs[10]

    def copies(p):
        cols = pl.ds(pl.multiple_of(p * PW, PW), PW)
        return [
            pltpu.make_async_copy(a.at[p], b.at[0, :, cols], sems.at[i, p])
            for i, (a, b) in enumerate(zip(sources, targets))
        ]

    def send(p, _):
        for copy in copies(p):
            copy.start()
        return 0

    def drain(p, _):
        for copy in copies(p):
            copy.wait()
        return 0

    lax.fori_loop(0, pairs, send, 0)
    result[...] = total[...]
    lax.fori_loop(0, pairs, drain, 0)


def body(ndp, nctx, queries, keys, values, out_grad, gain):
    _, length, width = queries.shape
    pairs = width // PW
    nsteps = (ndp - 1).bit_length() + (nctx - 1).bit_length()
    tile = pltpu.VMEM((pairs, length, PW), BF16)
    square = pltpu.VMEM((2, pairs, length, length), BF16)
    one = pltpu.VMEM((pairs, HD, HD), F32)
    two = pltpu.VMEM((2, pairs, HD, HD), F32)
    states = [two, one, one, one, one, one, one, two]
    hbm = pl.BlockSpec(memory_space=pl.ANY)
    vmem = pl.BlockSpec(memory_space=pltpu.VMEM)
    big = jax.ShapeDtypeStruct(queries.shape, BF16)
    out = pl.pallas_call(
        functools.partial(kernel, ndp, nctx, pairs),
        out_shape=(tile, tile, tile, tile, pltpu.VMEM((1, width), F32)),
        in_specs=[hbm, hbm, hbm, hbm, vmem],
        out_specs=(vmem, vmem, vmem, vmem, vmem),
        scratch_shapes=[
            tile, square, *states, *states,
            pltpu.VMEM((nsteps + 1, 1, width), F32),
            pltpu.VMEM((nsteps, 1, width), F32),
            pltpu.SemaphoreType.DMA((4, pairs)),
            pltpu.SemaphoreType.DMA((8,)),
            pltpu.SemaphoreType.DMA((8, pairs)),
            pltpu.SemaphoreType.DMA((nsteps,)),
            pltpu.SemaphoreType.DMA((nsteps,)),
        ],
        compiler_params=pltpu.CompilerParams(
            collective_id=0, has_side_effects=True, vmem_limit_bytes=44 << 20
        ),
        name="lightning",
    )(queries, keys, values, out_grad, gain.reshape(1, width))
    held = [pltpu.with_memory_space_constraint(a, pltpu.VMEM) for a in out]
    out = pl.pallas_call(
        functools.partial(settle, pairs),
        out_shape=(big, big, big, big, jax.ShapeDtypeStruct((1, width), F32)),
        in_specs=[vmem, vmem, vmem, vmem, vmem],
        out_specs=(hbm, hbm, hbm, hbm, vmem),
        scratch_shapes=[pltpu.SemaphoreType.DMA((4, pairs))],
        compiler_params=pltpu.CompilerParams(vmem_limit_bytes=2 << 20),
        name="settle",
    )(*held)
    return (*out[:4], out[4].reshape(width))


def solution(mesh):
    split = P("dp", "ctx", None)
    return jax.shard_map(
        functools.partial(body, mesh.shape["dp"], mesh.shape["ctx"]),
        mesh=mesh,
        in_specs=(split, split, split, split, P()),
        out_specs=(split, split, split, split, P()),
        check_vma=False,
    )
```

```python
import functools

import jax
import jax.numpy as jnp
from jax import lax
from jax.experimental import pallas as pl
from jax.experimental.pallas import tpu as pltpu
from jax.sharding import PartitionSpec as P

HD = 128
PW = 2 * HD
EPS = 1e-06
F32 = jnp.float32
BF16 = jnp.bfloat16
MESH = pl.DeviceIdType.MESH

LAG_PRO = 3
LAG_FWD = 2
LAG_COLUMN = 3
LAG_STEP = 5
LAG_ACROSS = 3
MIN_ACROSS = 9
LAG_FIN = 1
MIN_FIN = 17
GAIN_AT = 6
GAIN_STEP = 3


def nt(a, b):
    return lax.dot_general(a, b, (((1,), (1,)), ((), ())), preferred_element_type=F32)


def nn(a, b):
    return lax.dot_general(a, b, (((1,), (0,)), ((), ())), preferred_element_type=F32)


def tn(a, b):
    return lax.dot_general(a, b, (((0,), (0,)), ((), ())), preferred_element_type=F32)


def kernel(
    ndp, nctx, pairs,
    q_hbm, k_hbm, v_hbm, g_hbm, gain_ref,
    gb, qb, kb, vb, gg_ref,
    kept, held,
    s_all, x_in, c_out, y_in, e_in, e_out, p_out, p_all,
    t_all, tx_in, tc_out, ty_in, te_in, te_out, tp_out, tp_all,
    gsum, grecv,
    io_sem, send_sem, recv_sem, gs_sem, gr_sem,
):
    dp = lax.axis_index("dp")
    me = lax.axis_index("ctx")
    c = lax.rem(me, 2)
    y = lax.rem(me // 2, 2)
    z = me // 4
    nz = nctx // 4
    sib = (dp, me + 1 - 2 * c)
    ypeer = (dp, me + 2 - 4 * y)
    up = (dp, lax.min(me + 4, nctx - 1))
    down = (dp, lax.max(me - 4, 0))
    length = qb.shape[1]

    near = dp * 2 + c
    n_near = 2 * ndp
    gain_near = [lax.rem(near + r, n_near) for r in range(1, n_near)]
    gain_near = [(other // 2, me - c + lax.rem(other, 2)) for other in gain_near]
    gain_far = [lax.rem(z + r, nz) for r in range(1, nz)]
    gain_far = [(dp, me + 4 * (other - z)) for other in gain_far]

    def loads(p):
        cols = pl.ds(pl.multiple_of(p * PW, PW), PW)
        return [
            pltpu.make_async_copy(h.at[0, :, cols], b.at[p], io_sem.at[i, p])
            for i, (h, b) in enumerate(((k_hbm, kb), (v_hbm, vb), (q_hbm, qb), (g_hbm, gb)))
        ]

    def hop(kind, src, dst, p, to):
        return pltpu.make_async_remote_copy(
            src_ref=src, dst_ref=dst, send_sem=send_sem.at[kind], recv_sem=recv_sem.at[kind, p],
            device_id=to, device_id_type=MESH,
        )

    def load_kv(p, _):
        for copy in loads(p)[:2]:
            copy.start()
        return 0

    def load_qg(p, _):
        for copy in loads(p)[2:]:
            copy.start()
        return 0

    lax.fori_loop(0, pairs, load_kv, 0)
    lax.fori_loop(0, pairs, load_qg, 0)

    barrier = pltpu.get_barrier_semaphore()
    greet = gain_near + [ypeer] + gain_far
    for other in greet:
        pl.semaphore_signal(barrier, inc=1, device_id=other, device_id_type=MESH)
    pl.semaphore_wait(barrier, len(greet))

    @pl.when(z == 0)
    def _():
        e_in[...] = jnp.zeros_like(e_in)

    @pl.when(z == nz - 1)
    def _():
        te_in[...] = jnp.zeros_like(te_in)

    def to_chip(p, kind, all_ref, in_ref):
        return hop(kind, all_ref.at[1 - c, p], in_ref.at[p], p, sib)

    def chip_total(p):
        to_chip(p, 0, s_all, x_in).wait_recv()
        c_out[p] = s_all[c, p] + x_in[p]
        hop(1, c_out.at[p], y_in.at[p], p, ypeer).start()

    def along(p):
        hop(1, c_out.at[p], y_in.at[p], p, ypeer).wait_recv()

        @pl.when(z != 0)
        def _():
            hop(2, e_out.at[p], e_in.at[p], p, up).wait_recv()

        entering = e_in[p]
        other = y_in[p]

        @pl.when(z != nz - 1)
        def _():
            e_out[p] = entering + (c_out[p] + other)
            hop(2, e_out.at[p], e_in.at[p], p, up).start()

        base = entering + jnp.where(y == 1, other, 0.0)
        p_out[p] = base + jnp.where(c == 1, 0.0, s_all[c, p])
        hop(3, p_out.at[p], p_all.at[c, p], p, sib).start()
        p_all[c, p] = base + jnp.where(c == 1, x_in[p], 0.0)

    def column(p):
        to_chip(p, 4, t_all, tx_in).wait_recv()
        own = t_all[c, p] + tx_in[p]

        @pl.when(z != nz - 1)
        def _():
            hop(6, te_out.at[p], te_in.at[p], p, down).wait_recv()

        entering = te_in[p]
        leaving = entering + own
        te_out[p] = leaving

        @pl.when(z != 0)
        def _():
            hop(6, te_out.at[p], te_in.at[p], p, down).start()

        tc_out[p] = jnp.where(y == 1, leaving, entering)
        hop(5, tc_out.at[p], ty_in.at[p], p, ypeer).start()

    def across(p):
        hop(5, tc_out.at[p], ty_in.at[p], p, ypeer).wait_recv()
        base = te_in[p] + ty_in[p]
        tp_out[p] = base + jnp.where(c == 0, 0.0, t_all[c, p])
        hop(7, tp_out.at[p], tp_all.at[c, p], p, sib).start()
        tp_all[c, p] = base + jnp.where(c == 0, tx_in[p], 0.0)

    def prologue(t, _):
        @pl.when(t < pairs)
        def _():
            for copy in loads(t)[:2]:
                copy.wait()
            for j in range(2):
                at = slice(j * HD, (j + 1) * HD)
                s_all[j, t] = tn(kb[t, :, at], vb[t, :, at])
            to_chip(t, 0, s_all, x_in).start()

        @pl.when(t >= LAG_PRO)
        def _():
            chip_total(t - LAG_PRO)
        return 0

    lax.fori_loop(0, pairs + LAG_PRO, prologue, 0)

    def forward(p):
        for copy in loads(p)[2:]:
            copy.wait()
        hop(3, p_out.at[p], p_all.at[1 - c, p], p, sib).wait_recv()
        row = lax.broadcasted_iota(jnp.int32, (length, length), 0)
        col = lax.broadcasted_iota(jnp.int32, (length, length), 1)
        causal = row >= col
        two = range(2)
        at = [slice(j * HD, (j + 1) * HD) for j in two]
        lanes = [pl.ds(pl.multiple_of(p * PW + j * HD, HD), HD) for j in two]
        query = [qb[p, :, at[j]] for j in two]
        key_rows = [kb[p, :, at[j]] for j in two]
        value = [vb[p, :, at[j]] for j in two]
        grad = [gb[p, :, at[j]].astype(F32) for j in two]
        prefix = [p_all[j, p].astype(BF16) for j in two]
        gain = [gain_ref[:, lanes[j]] for j in two]
        scores = [jnp.where(causal, nt(query[j], key_rows[j]), 0.0).astype(BF16) for j in two]
        attended = [
            nn(
                jnp.concatenate([scores[j], query[j]], axis=1),
                jnp.concatenate([value[j], prefix[j]], axis=0),
            )
            for j in two
        ]
        inverse = [
            lax.rsqrt(jnp.mean(attended[j] * attended[j], axis=-1, keepdims=True) + EPS) for j in two
        ]
        normed = [attended[j] * inverse[j] for j in two]
        product = [grad[j] * normed[j] for j in two]
        mean = [jnp.mean(product[j] * gain[j], axis=-1, keepdims=True) for j in two]
        dattn = [
            (inverse[j] * (grad[j] * gain[j] - normed[j] * mean[j])).astype(BF16) for j in two
        ]
        gstate = [tn(query[j], dattn[j]) for j in two]
        for j in two:
            t_all[j, p] = gstate[j]
        to_chip(p, 4, t_all, tx_in).start()
        for j in two:
            kept[p, :, at[j]] = dattn[j]
            held[j, p] = scores[j]
            gsum[0, :, lanes[j]] = jnp.sum(product[j], axis=0, keepdims=True)
            gb[p, :, at[j]] = (normed[j] * gain[j]).astype(BF16)

    def final(p):
        hop(7, tp_out.at[p], tp_all.at[1 - c, p], p, sib).wait_recv()
        row = lax.broadcasted_iota(jnp.int32, (length, length), 0)
        col = lax.broadcasted_iota(jnp.int32, (length, length), 1)
        causal = row >= col
        two = range(2)
        at = [slice(j * HD, (j + 1) * HD) for j in two]
        query = [qb[p, :, at[j]] for j in two]
        key_rows = [kb[p, :, at[j]] for j in two]
        value = [vb[p, :, at[j]] for j in two]
        dattn = [kept[p, :, at[j]] for j in two]
        prefix = [p_all[j, p].astype(BF16) for j in two]
        suffix = [tp_all[j, p].astype(BF16) for j in two]
        dscore = [jnp.where(causal, nt(dattn[j], value[j]), 0.0).astype(BF16) for j in two]
        grad_v = [
            (tn(held[j, p], dattn[j]) + nn(key_rows[j], suffix[j])).astype(BF16) for j in two
        ]
        grad_q = [
            nn(
                jnp.concatenate([dscore[j], dattn[j]], axis=1),
                jnp.concatenate([key_rows[j], prefix[j].T], axis=0),
            ).astype(BF16)
            for j in two
        ]
        grad_k = [
            (tn(dscore[j], query[j]) + nt(value[j], suffix[j])).astype(BF16) for j in two
        ]
        for j in two:
            qb[p, :, at[j]] = grad_q[j]
            kb[p, :, at[j]] = grad_k[j]
            vb[p, :, at[j]] = grad_v[j]

    def gain_copy(level, lane, source, to):
        return pltpu.make_async_remote_copy(
            src_ref=gsum.at[level], dst_ref=grecv.at[level, source],
            send_sem=gs_sem.at[level, lane], recv_sem=gr_sem.at[level, source],
            device_id=to, device_id_type=MESH,
        )

    levels = [(near, n_near, gain_near), (z, nz, gain_far), (y, 2, [ypeer])]

    def gain_send(level):
        source, count, others = levels[level]
        grecv[level, source] = gsum[level]
        for lane, other in enumerate(others):
            gain_copy(level, lane, source, other).start()

    def gain_take(level):
        source, count, others = levels[level]
        for r in range(1, count):
            gain_copy(level, 0, lax.rem(source + r, count), others[0]).wait_recv()
        sum_ = grecv[level, 0]
        for r in range(1, count):
            sum_ = sum_ + grecv[level, r]
        gsum[level + 1] = sum_

    def lags(behind):
        column_lag = LAG_COLUMN + LAG_STEP * behind
        across_lag = lax.max(column_lag + LAG_ACROSS, MIN_ACROSS)
        return column_lag, across_lag, lax.max(across_lag + LAG_FIN, MIN_FIN)

    lag_column, lag_across, lag_fin = lags(nz - 1 - z)
    gain_at = lax.max(lag_fin + GAIN_AT, pairs + LAG_FWD)
    most = max(LAG_COLUMN + LAG_STEP * (nz - 1) + LAG_ACROSS, MIN_ACROSS) + LAG_FIN
    most = max(most, MIN_FIN)
    total = max(pairs + most, max(most + GAIN_AT, pairs + LAG_FWD) + 2 * GAIN_STEP + 1)

    def guarded(p, stage):
        @pl.when(jnp.logical_and(p >= 0, p < pairs))
        def _():
            stage(p)

    def main(t, _):
        guarded(t - LAG_FWD, forward)
        guarded(t - lag_column, column)
        guarded(t - lag_across, across)
        guarded(t, along)
        guarded(t - lag_fin, final)

        @pl.when(t == gain_at)
        def _():
            gain_send(0)

        @pl.when(t == gain_at + GAIN_STEP)
        def _():
            gain_take(0)
            gain_send(1)

        @pl.when(t == gain_at + 2 * GAIN_STEP)
        def _():
            gain_take(1)
            gain_send(2)
        return 0

    lax.fori_loop(0, total, main, 0)
    gain_take(2)
    gg_ref[...] = gsum[3]

    for level in range(3):
        source, count, others = levels[level]
        for lane, other in enumerate(others):
            gain_copy(level, lane, source, other).wait_send()
    for kind, all_ref, in_ref, out_ref, y_ref, eo_ref, e_ref, po_ref, pa_ref in (
        (0, s_all, x_in, c_out, y_in, e_out, e_in, p_out, p_all),
        (4, t_all, tx_in, tc_out, ty_in, te_out, te_in, tp_out, tp_all),
    ):
        hop(kind, all_ref.at[1 - c], in_ref, 0, sib).wait_send()
        hop(kind + 1, out_ref, y_ref, 0, ypeer).wait_send()
        reverse = kind == 4

        @pl.when(z != (0 if reverse else nz - 1))
        def _():
            hop(kind + 2, eo_ref, e_ref, 0, down if reverse else up).wait_send()

        hop(kind + 3, po_ref, pa_ref.at[c], 0, sib).wait_send()


def settle(pairs, *refs):
    sources, total, targets, result, sems = refs[:4], refs[4], refs[5:9], refs[9], refs[10]

    def copies(p):
        cols = pl.ds(pl.multiple_of(p * PW, PW), PW)
        return [
            pltpu.make_async_copy(a.at[p], b.at[0, :, cols], sems.at[i, p])
            for i, (a, b) in enumerate(zip(sources, targets))
        ]

    def send(p, _):
        for copy in copies(p):
            copy.start()
        return 0

    def drain(p, _):
        for copy in copies(p):
            copy.wait()
        return 0

    lax.fori_loop(0, pairs, send, 0)
    result[...] = total[...]
    lax.fori_loop(0, pairs, drain, 0)


def body(ndp, nctx, queries, keys, values, out_grad, gain):
    _, length, width = queries.shape
    pairs = width // PW
    most = max(2 * ndp, 2, nctx // 4)
    tile = pltpu.VMEM((pairs, length, PW), BF16)
    square = pltpu.VMEM((2, pairs, length, length), BF16)
    one = pltpu.VMEM((pairs, HD, HD), F32)
    two = pltpu.VMEM((2, pairs, HD, HD), F32)
    states = [two, one, one, one, one, one, one, two]
    hbm = pl.BlockSpec(memory_space=pl.ANY)
    vmem = pl.BlockSpec(memory_space=pltpu.VMEM)
    big = jax.ShapeDtypeStruct(queries.shape, BF16)
    out = pl.pallas_call(
        functools.partial(kernel, ndp, nctx, pairs),
        out_shape=(tile, tile, tile, tile, pltpu.VMEM((1, width), F32)),
        in_specs=[hbm, hbm, hbm, hbm, vmem],
        out_specs=(vmem, vmem, vmem, vmem, vmem),
        scratch_shapes=[
            tile, square, *states, *states,
            pltpu.VMEM((4, 1, width), F32),
            pltpu.VMEM((3, most, 1, width), F32),
            pltpu.SemaphoreType.DMA((4, pairs)),
            pltpu.SemaphoreType.DMA((8,)),
            pltpu.SemaphoreType.DMA((8, pairs)),
            pltpu.SemaphoreType.DMA((3, most)),
            pltpu.SemaphoreType.DMA((3, most)),
        ],
        compiler_params=pltpu.CompilerParams(
            collective_id=0, has_side_effects=True, vmem_limit_bytes=44 << 20
        ),
        name="lightning",
    )(queries, keys, values, out_grad, gain.reshape(1, width))
    held = [pltpu.with_memory_space_constraint(a, pltpu.VMEM) for a in out]
    out = pl.pallas_call(
        functools.partial(settle, pairs),
        out_shape=(big, big, big, big, jax.ShapeDtypeStruct((1, width), F32)),
        in_specs=[vmem, vmem, vmem, vmem, vmem],
        out_specs=(hbm, hbm, hbm, hbm, vmem),
        scratch_shapes=[pltpu.SemaphoreType.DMA((4, pairs))],
        compiler_params=pltpu.CompilerParams(vmem_limit_bytes=2 << 20),
        name="settle",
    )(*held)
    return (*out[:4], out[4].reshape(width))


def solution(mesh):
    split = P("dp", "ctx", None)
    return jax.shard_map(
        functools.partial(body, mesh.shape["dp"], mesh.shape["ctx"]),
        mesh=mesh,
        in_specs=(split, split, split, split, P()),
        out_specs=(split, split, split, split, P()),
        check_vma=False,
    )
```

```python
import functools

import jax
import jax.numpy as jnp
from jax import lax
from jax.experimental import pallas as pl
from jax.experimental.pallas import tpu as pltpu
from jax.sharding import PartitionSpec as P

HD = 128
PW = 2 * HD
ROWS = 128
EPS = 1e-06
F32 = jnp.float32
BF16 = jnp.bfloat16
MESH = pl.DeviceIdType.MESH

PEEL = 2
LAG_PRO = 3
HEAD_AT = 9
HEAD_STEP = 3
LAG_FWD = 2
LAG_COLUMN = 3
LAG_STEP = 5
LAG_ACROSS = 3
MIN_ACROSS = 9
LAG_FIN = 1
MIN_FIN = 17
GAIN_AT = 6
GAIN_STEP = 3


def nt(a, b):
    return lax.dot_general(a, b, (((1,), (1,)), ((), ())), preferred_element_type=F32)


def nn(a, b):
    return lax.dot_general(a, b, (((1,), (0,)), ((), ())), preferred_element_type=F32)


def tn(a, b):
    return lax.dot_general(a, b, (((0,), (0,)), ((), ())), preferred_element_type=F32)


def lower(a, b):
    length = a.shape[0]
    row = lax.broadcasted_iota(jnp.int32, (ROWS, ROWS), 0)
    col = lax.broadcasted_iota(jnp.int32, (ROWS, ROWS), 1)
    strips = []
    for at in range(0, length, ROWS):
        strip = nt(a[at:at + ROWS], b[:at + ROWS])
        last = jnp.where(row >= col, strip[:, at:], 0.0)
        if at:
            last = jnp.concatenate([strip[:, :at], last], axis=1)
        strips.append(last.astype(BF16))
    return strips


def by_rows(strips, left, right, tail):
    out = []
    for i, strip in enumerate(strips):
        at = i * ROWS
        out.append(
            nn(
                jnp.concatenate([strip, left[at:at + ROWS]], axis=1),
                jnp.concatenate([right[:at + ROWS], tail], axis=0),
            )
        )
    return jnp.concatenate(out, axis=0)


def by_columns(strips, left, right, tail):
    out = []
    for j in range(len(strips)):
        at = j * ROWS
        column = jnp.concatenate([strip[:, at:at + ROWS] for strip in strips[j:]], axis=0)
        out.append(
            nn(
                jnp.concatenate([column.T, left[at:at + ROWS]], axis=1),
                jnp.concatenate([right[at:], tail], axis=0),
            )
        )
    return jnp.concatenate(out, axis=0)


def kernel(
    ndp, nctx, pairs,
    q_hbm, k_hbm, v_hbm, g_hbm, gain_ref,
    gb, qb, kb, vb, gg_ref,
    kept, held,
    s_all, x_in, c_out, y_in, e_in, e_out, p_out, p_all,
    t_all, tx_in, tc_out, ty_in, te_in, te_out, tp_out, tp_all,
    gsum, grecv,
    io_sem, send_sem, recv_sem, gs_sem, gr_sem,
):
    dp = lax.axis_index("dp")
    me = lax.axis_index("ctx")
    c = lax.rem(me, 2)
    y = lax.rem(me // 2, 2)
    z = me // 4
    nz = nctx // 4
    sib = (dp, me + 1 - 2 * c)
    ypeer = (dp, me + 2 - 4 * y)
    up = (dp, lax.min(me + 4, nctx - 1))
    down = (dp, lax.max(me - 4, 0))
    length = qb.shape[1]

    near = dp * 2 + c
    n_near = 2 * ndp
    gain_near = [lax.rem(near + r, n_near) for r in range(1, n_near)]
    gain_near = [(other // 2, me - c + lax.rem(other, 2)) for other in gain_near]
    gain_far = [lax.rem(z + r, nz) for r in range(1, nz)]
    gain_far = [(dp, me + 4 * (other - z)) for other in gain_far]

    barrier = pltpu.get_barrier_semaphore()
    greet = gain_near + [ypeer] + gain_far
    for other in greet:
        pl.semaphore_signal(barrier, inc=1, device_id=other, device_id_type=MESH)

    def loads(p):
        cols = pl.ds(pl.multiple_of(p * PW, PW), PW)
        return [
            pltpu.make_async_copy(h.at[0, :, cols], b.at[p], io_sem.at[i, p])
            for i, (h, b) in enumerate(((k_hbm, kb), (v_hbm, vb), (q_hbm, qb), (g_hbm, gb)))
        ]

    def hop(kind, src, dst, p, to):
        return pltpu.make_async_remote_copy(
            src_ref=src, dst_ref=dst, send_sem=send_sem.at[kind], recv_sem=recv_sem.at[kind, p],
            device_id=to, device_id_type=MESH,
        )

    def load_kv(p, _):
        for copy in loads(p)[:2]:
            copy.start()
        return 0

    def load_qg(p, _):
        for copy in loads(p)[2:]:
            copy.start()
        return 0

    lax.fori_loop(0, pairs, load_kv, 0)
    lax.fori_loop(0, pairs, load_qg, 0)


    @pl.when(z == 0)
    def _():
        e_in[...] = jnp.zeros_like(e_in)

    @pl.when(z == nz - 1)
    def _():
        te_in[...] = jnp.zeros_like(te_in)

    def to_chip(p, kind, all_ref, in_ref):
        return hop(kind, all_ref.at[1 - c, p], in_ref.at[p], p, sib)

    def z_hop(kind, src, dst, p, half, to):
        rows = pl.ds(half * (HD // 2), HD // 2)
        lane = kind if half == 0 else 8 + kind // 4
        return pltpu.make_async_remote_copy(
            src_ref=src.at[p, rows], dst_ref=dst.at[p, rows],
            send_sem=send_sem.at[lane], recv_sem=recv_sem.at[lane, p],
            device_id=to, device_id_type=MESH,
        )

    def chip_total(p):
        to_chip(p, 0, s_all, x_in).wait_recv()
        c_out[p] = s_all[c, p] + x_in[p]
        hop(1, c_out.at[p], y_in.at[p], p, ypeer).start()

    def along(p):
        hop(1, c_out.at[p], y_in.at[p], p, ypeer).wait_recv()

        for half in range(2):
            rows = slice(half * (HD // 2), (half + 1) * (HD // 2))

            @pl.when(z != 0)
            def _():
                z_hop(2, e_out, e_in, p, half, up).wait_recv()

            @pl.when(z != nz - 1)
            def _():
                e_out[p, rows] = e_in[p, rows] + (c_out[p, rows] + y_in[p, rows])
                z_hop(2, e_out, e_in, p, half, up).start()

        entering = e_in[p]
        other = y_in[p]
        base = entering + jnp.where(y == 1, other, 0.0)
        p_out[p] = base + jnp.where(c == 1, 0.0, s_all[c, p])
        hop(3, p_out.at[p], p_all.at[c, p], p, sib).start()
        p_all[c, p] = base + jnp.where(c == 1, x_in[p], 0.0)

    def column(p):
        to_chip(p, 4, t_all, tx_in).wait_recv()
        for half in range(2):
            rows = slice(half * (HD // 2), (half + 1) * (HD // 2))
            own = t_all[c, p, rows] + tx_in[p, rows]

            @pl.when(z != nz - 1)
            def _():
                z_hop(6, te_out, te_in, p, half, down).wait_recv()

            entering = te_in[p, rows]
            leaving = entering + own
            te_out[p, rows] = leaving

            @pl.when(z != 0)
            def _():
                z_hop(6, te_out, te_in, p, half, down).start()

            tc_out[p, rows] = jnp.where(y == 1, leaving, entering)
        hop(5, tc_out.at[p], ty_in.at[p], p, ypeer).start()

    def across(p):
        hop(5, tc_out.at[p], ty_in.at[p], p, ypeer).wait_recv()
        base = te_in[p] + ty_in[p]
        tp_out[p] = base + jnp.where(c == 0, 0.0, t_all[c, p])
        hop(7, tp_out.at[p], tp_all.at[c, p], p, sib).start()
        tp_all[c, p] = base + jnp.where(c == 0, tx_in[p], 0.0)

    def state(t):
        for copy in loads(t)[:2]:
            copy.wait()
        for j in range(2):
            at = slice(j * HD, (j + 1) * HD)
            s_all[j, t] = tn(kb[t, :, at], vb[t, :, at])

    def prologue(t, _):
        @pl.when(t < pairs)
        def _():
            @pl.when(t >= PEEL)
            def _():
                state(t)
            to_chip(t, 0, s_all, x_in).start()

        @pl.when(t >= LAG_PRO)
        def _():
            chip_total(t - LAG_PRO)

        ahead = t - HEAD_AT

        @pl.when((z == 0) & (ahead >= 0) & (lax.rem(ahead, HEAD_STEP) == 0))
        def _():
            along(ahead // HEAD_STEP)
        return 0

    for t in range(PEEL):
        state(t)
    pl.semaphore_wait(barrier, len(greet))
    lax.fori_loop(0, pairs + LAG_PRO, prologue, 0)

    def forward(p):
        for copy in loads(p)[2:]:
            copy.wait()
        hop(3, p_out.at[p], p_all.at[1 - c, p], p, sib).wait_recv()
        two = range(2)
        at = [slice(j * HD, (j + 1) * HD) for j in two]
        lanes = [pl.ds(pl.multiple_of(p * PW + j * HD, HD), HD) for j in two]
        query = [qb[p, :, at[j]] for j in two]
        key_rows = [kb[p, :, at[j]] for j in two]
        value = [vb[p, :, at[j]] for j in two]
        grad = [gb[p, :, at[j]].astype(F32) for j in two]
        prefix = [p_all[j, p].astype(BF16) for j in two]
        gain = [gain_ref[:, lanes[j]] for j in two]
        scores = [lower(query[j], key_rows[j]) for j in two]
        attended = [by_rows(scores[j], query[j], value[j], prefix[j]) for j in two]
        inverse = [
            lax.rsqrt(jnp.mean(attended[j] * attended[j], axis=-1, keepdims=True) + EPS) for j in two
        ]
        normed = [attended[j] * inverse[j] for j in two]
        product = [grad[j] * normed[j] for j in two]
        mean = [jnp.mean(product[j] * gain[j], axis=-1, keepdims=True) for j in two]
        dattn = [
            (inverse[j] * (grad[j] * gain[j] - normed[j] * mean[j])).astype(BF16) for j in two
        ]
        gstate = [tn(query[j], dattn[j]) for j in two]
        for j in two:
            t_all[j, p] = gstate[j]
        to_chip(p, 4, t_all, tx_in).start()
        for j in two:
            kept[p, :, at[j]] = dattn[j]
            for i, strip in enumerate(scores[j]):
                held[j, p, i * ROWS:(i + 1) * ROWS, :(i + 1) * ROWS] = strip
            gsum[0, :, lanes[j]] = jnp.sum(product[j], axis=0, keepdims=True)
            gb[p, :, at[j]] = (normed[j] * gain[j]).astype(BF16)

    def final(p):
        hop(7, tp_out.at[p], tp_all.at[1 - c, p], p, sib).wait_recv()
        two = range(2)
        at = [slice(j * HD, (j + 1) * HD) for j in two]
        query = [qb[p, :, at[j]] for j in two]
        key_rows = [kb[p, :, at[j]] for j in two]
        value = [vb[p, :, at[j]] for j in two]
        dattn = [kept[p, :, at[j]] for j in two]
        prefix = [p_all[j, p].astype(BF16) for j in two]
        suffix = [tp_all[j, p].astype(BF16) for j in two]
        dscore = [lower(dattn[j], value[j]) for j in two]
        scores = [
            [held[j, p, at_:at_ + ROWS, :at_ + ROWS] for at_ in range(0, length, ROWS)] for j in two
        ]
        grad_v = [by_columns(scores[j], key_rows[j], dattn[j], suffix[j]).astype(BF16) for j in two]
        grad_q = [by_rows(dscore[j], dattn[j], key_rows[j], prefix[j].T).astype(BF16) for j in two]
        grad_k = [by_columns(dscore[j], value[j], query[j], suffix[j].T).astype(BF16) for j in two]
        for j in two:
            qb[p, :, at[j]] = grad_q[j]
            kb[p, :, at[j]] = grad_k[j]
            vb[p, :, at[j]] = grad_v[j]

    def gain_copy(level, lane, source, to):
        return pltpu.make_async_remote_copy(
            src_ref=gsum.at[level], dst_ref=grecv.at[level, source],
            send_sem=gs_sem.at[level, lane], recv_sem=gr_sem.at[level, source],
            device_id=to, device_id_type=MESH,
        )

    levels = [(near, n_near, gain_near), (z, nz, gain_far), (y, 2, [ypeer])]

    def gain_send(level):
        source, count, others = levels[level]
        grecv[level, source] = gsum[level]
        for lane, other in enumerate(others):
            gain_copy(level, lane, source, other).start()

    def gain_take(level):
        source, count, others = levels[level]
        for r in range(1, count):
            gain_copy(level, 0, lax.rem(source + r, count), others[0]).wait_recv()
        sum_ = grecv[level, 0]
        for r in range(1, count):
            sum_ = sum_ + grecv[level, r]
        gsum[level + 1] = sum_

    def lags(behind):
        column_lag = LAG_COLUMN + LAG_STEP * behind
        across_lag = lax.max(column_lag + LAG_ACROSS, MIN_ACROSS)
        return column_lag, across_lag, lax.max(across_lag + LAG_FIN, MIN_FIN)

    lag_column, lag_across, lag_fin = lags(nz - 1 - z)
    gain_at = lax.max(lag_fin + GAIN_AT, pairs + LAG_FWD)
    most = max(LAG_COLUMN + LAG_STEP * (nz - 1) + LAG_ACROSS, MIN_ACROSS) + LAG_FIN
    most = max(most, MIN_FIN)
    total = max(pairs + most, max(most + GAIN_AT, pairs + LAG_FWD) + 2 * GAIN_STEP + 1)

    head = jnp.where(z == 0, (pairs + LAG_PRO - HEAD_AT + HEAD_STEP - 1) // HEAD_STEP, 0)

    def guarded(p, stage, first=0):
        @pl.when(jnp.logical_and(p >= first, p < pairs))
        def _():
            stage(p)

    def main(t, _):
        guarded(t - LAG_FWD, forward)
        guarded(t - lag_column, column)
        guarded(t - lag_across, across)
        guarded(t, along, head)
        guarded(t - lag_fin, final)

        @pl.when(t == gain_at)
        def _():
            gain_send(0)

        @pl.when(t == gain_at + GAIN_STEP)
        def _():
            gain_take(0)
            gain_send(1)

        @pl.when(t == gain_at + 2 * GAIN_STEP)
        def _():
            gain_take(1)
            gain_send(2)
        return 0

    lax.fori_loop(0, total, main, 0)
    gain_take(2)
    gg_ref[...] = gsum[3]

    for level in range(3):
        source, count, others = levels[level]
        for lane, other in enumerate(others):
            gain_copy(level, lane, source, other).wait_send()
    for kind, all_ref, in_ref, out_ref, y_ref, eo_ref, e_ref, po_ref, pa_ref in (
        (0, s_all, x_in, c_out, y_in, e_out, e_in, p_out, p_all),
        (4, t_all, tx_in, tc_out, ty_in, te_out, te_in, tp_out, tp_all),
    ):
        hop(kind, all_ref.at[1 - c], in_ref, 0, sib).wait_send()
        hop(kind + 1, out_ref, y_ref, 0, ypeer).wait_send()
        reverse = kind == 4

        @pl.when(z != (0 if reverse else nz - 1))
        def _():
            for half in range(2):
                rows = pl.ds(half * (HD // 2), HD // 2)
                pltpu.make_async_remote_copy(
                    src_ref=eo_ref.at[:, rows], dst_ref=e_ref.at[:, rows],
                    send_sem=send_sem.at[(kind + 2) if half == 0 else 8 + kind // 4],
                    recv_sem=recv_sem.at[0, 0],
                    device_id=down if reverse else up, device_id_type=MESH,
                ).wait_send()

        hop(kind + 3, po_ref, pa_ref.at[c], 0, sib).wait_send()


def settle(pairs, *refs):
    sources, total, targets, result, sems = refs[:4], refs[4], refs[5:9], refs[9], refs[10]

    def copies(p):
        cols = pl.ds(pl.multiple_of(p * PW, PW), PW)
        return [
            pltpu.make_async_copy(a.at[p], b.at[0, :, cols], sems.at[i, p])
            for i, (a, b) in enumerate(zip(sources, targets))
        ]

    def send(p, _):
        for copy in copies(p):
            copy.start()
        return 0

    def drain(p, _):
        for copy in copies(p):
            copy.wait()
        return 0

    lax.fori_loop(0, pairs, send, 0)
    result[...] = total[...]
    lax.fori_loop(0, pairs, drain, 0)


def body(ndp, nctx, queries, keys, values, out_grad, gain):
    _, length, width = queries.shape
    pairs = width // PW
    most = max(2 * ndp, 2, nctx // 4)
    tile = pltpu.VMEM((pairs, length, PW), BF16)
    square = pltpu.VMEM((2, pairs, length, length), BF16)
    one = pltpu.VMEM((pairs, HD, HD), F32)
    two = pltpu.VMEM((2, pairs, HD, HD), F32)
    states = [two, one, one, one, one, one, one, two]
    hbm = pl.BlockSpec(memory_space=pl.ANY)
    vmem = pl.BlockSpec(memory_space=pltpu.VMEM)
    big = jax.ShapeDtypeStruct(queries.shape, BF16)
    out = pl.pallas_call(
        functools.partial(kernel, ndp, nctx, pairs),
        out_shape=(tile, tile, tile, tile, pltpu.VMEM((1, width), F32)),
        in_specs=[hbm, hbm, hbm, hbm, vmem],
        out_specs=(vmem, vmem, vmem, vmem, vmem),
        scratch_shapes=[
            tile, square, *states, *states,
            pltpu.VMEM((4, 1, width), F32),
            pltpu.VMEM((3, most, 1, width), F32),
            pltpu.SemaphoreType.DMA((4, pairs)),
            pltpu.SemaphoreType.DMA((10,)),
            pltpu.SemaphoreType.DMA((10, pairs)),
            pltpu.SemaphoreType.DMA((3, most)),
            pltpu.SemaphoreType.DMA((3, most)),
        ],
        compiler_params=pltpu.CompilerParams(
            collective_id=0, has_side_effects=True, vmem_limit_bytes=44 << 20
        ),
        name="lightning",
    )(queries, keys, values, out_grad, gain.reshape(1, width))
    held = [pltpu.with_memory_space_constraint(a, pltpu.VMEM) for a in out]
    out = pl.pallas_call(
        functools.partial(settle, pairs),
        out_shape=(big, big, big, big, jax.ShapeDtypeStruct((1, width), F32)),
        in_specs=[vmem, vmem, vmem, vmem, vmem],
        out_specs=(hbm, hbm, hbm, hbm, vmem),
        scratch_shapes=[pltpu.SemaphoreType.DMA((4, pairs))],
        compiler_params=pltpu.CompilerParams(vmem_limit_bytes=2 << 20),
        name="settle",
    )(*held)
    return (*out[:4], out[4].reshape(width))


def solution(mesh):
    split = P("dp", "ctx", None)
    return jax.shard_map(
        functools.partial(body, mesh.shape["dp"], mesh.shape["ctx"]),
        mesh=mesh,
        in_specs=(split, split, split, split, P()),
        out_specs=(split, split, split, split, P()),
        check_vma=False,
    )
```

```python
import functools

import jax
import jax.numpy as jnp
from jax import lax
from jax.experimental import pallas as pl
from jax.experimental.pallas import tpu as pltpu
from jax.sharding import PartitionSpec as P

HD = 128
PW = 2 * HD
ROWS = 128
EPS = 1e-06
F32 = jnp.float32
BF16 = jnp.bfloat16
MESH = pl.DeviceIdType.MESH

PEEL = 2
LAG_PRO = 2
HEAD_AT = 9
HEAD_STEP = 3
LAG_FWD = 2
LAG_COLUMN = 3
LAG_STEP = 5
LAG_ACROSS = 3
MIN_ACROSS = 9
LAG_FIN = 1
MIN_FIN = 17
GAIN_AT = 6
GAIN_STEP = 3
LATE = 4


def nt(a, b):
    return lax.dot_general(a, b, (((1,), (1,)), ((), ())), preferred_element_type=F32)


def nn(a, b):
    return lax.dot_general(a, b, (((1,), (0,)), ((), ())), preferred_element_type=F32)


def tn(a, b):
    return lax.dot_general(a, b, (((0,), (0,)), ((), ())), preferred_element_type=F32)


def lower(a, b):
    length = a.shape[0]
    row = lax.broadcasted_iota(jnp.int32, (ROWS, ROWS), 0)
    col = lax.broadcasted_iota(jnp.int32, (ROWS, ROWS), 1)
    strips = []
    for at in range(0, length, ROWS):
        strip = nt(a[at:at + ROWS], b[:at + ROWS])
        last = jnp.where(row >= col, strip[:, at:], 0.0)
        if at:
            last = jnp.concatenate([strip[:, :at], last], axis=1)
        strips.append(last.astype(BF16))
    return strips


def by_rows(strips, left, right, tail):
    out = []
    for i, strip in enumerate(strips):
        at = i * ROWS
        out.append(
            nn(
                jnp.concatenate([strip, left[at:at + ROWS]], axis=1),
                jnp.concatenate([right[:at + ROWS], tail], axis=0),
            )
        )
    return jnp.concatenate(out, axis=0)


def by_columns(strips, left, right, tail):
    out = []
    for j in range(len(strips)):
        at = j * ROWS
        column = jnp.concatenate([strip[:, at:at + ROWS] for strip in strips[j:]], axis=0)
        out.append(
            nn(
                jnp.concatenate([column.T, left[at:at + ROWS]], axis=1),
                jnp.concatenate([right[at:], tail], axis=0),
            )
        )
    return jnp.concatenate(out, axis=0)


def gradients(p, qs, ks, vs, kept, held, prefixes, suffixes, at_state, targets, at_target):
    length = qs.shape[1]
    two = range(2)
    at = [slice(j * HD, (j + 1) * HD) for j in two]
    query = [qs[p, :, at[j]] for j in two]
    key_rows = [ks[p, :, at[j]] for j in two]
    value = [vs[p, :, at[j]] for j in two]
    dattn = [kept[p, :, at[j]] for j in two]
    prefix = [prefixes[j, at_state].astype(BF16) for j in two]
    suffix = [suffixes[j, at_state].astype(BF16) for j in two]
    dscore = [lower(dattn[j], value[j]) for j in two]
    scores = [
        [held[j, p, row:row + ROWS, :row + ROWS] for row in range(0, length, ROWS)] for j in two
    ]
    grad_v = [by_columns(scores[j], key_rows[j], dattn[j], suffix[j]).astype(BF16) for j in two]
    grad_q = [by_rows(dscore[j], dattn[j], key_rows[j], prefix[j].T).astype(BF16) for j in two]
    grad_k = [by_columns(dscore[j], value[j], query[j], suffix[j].T).astype(BF16) for j in two]
    for j in two:
        for target, value_ in zip(targets, (grad_q, grad_k, grad_v)):
            target[at_target, :, at[j]] = value_[j]


def kernel(
    ndp, nctx, pairs,
    q_hbm, k_hbm, v_hbm, g_hbm, gain_ref,
    gb, qb, kb, vb, gg_ref, kept, held, prefix_out, suffix_out,

    s_all, x_in, c_out, y_in, e_in, e_out, p_out, p_all,
    t_all, tx_in, tc_out, ty_in, te_in, te_out, tp_out, tp_all,
    gsum, grecv,
    io_sem, send_sem, recv_sem, gs_sem, gr_sem,
):
    dp = lax.axis_index("dp")
    me = lax.axis_index("ctx")
    c = lax.rem(me, 2)
    y = lax.rem(me // 2, 2)
    z = me // 4
    nz = nctx // 4
    sib = (dp, me + 1 - 2 * c)
    ypeer = (dp, me + 2 - 4 * y)
    up = (dp, lax.min(me + 4, nctx - 1))
    down = (dp, lax.max(me - 4, 0))
    length = qb.shape[1]

    near = dp * 2 + c
    n_near = 2 * ndp
    gain_near = [lax.rem(near + r, n_near) for r in range(1, n_near)]
    gain_near = [(other // 2, me - c + lax.rem(other, 2)) for other in gain_near]
    gain_far = [lax.rem(z + r, nz) for r in range(1, nz)]
    gain_far = [(dp, me + 4 * (other - z)) for other in gain_far]

    barrier = pltpu.get_barrier_semaphore()
    greet = gain_near + [ypeer] + gain_far
    for other in greet:
        pl.semaphore_signal(barrier, inc=1, device_id=other, device_id_type=MESH)

    def loads(p):
        cols = pl.ds(pl.multiple_of(p * PW, PW), PW)
        return [
            pltpu.make_async_copy(h.at[0, :, cols], b.at[p], io_sem.at[i, p])
            for i, (h, b) in enumerate(((k_hbm, kb), (v_hbm, vb), (q_hbm, qb), (g_hbm, gb)))
        ]

    def hop(kind, src, dst, p, to):
        return pltpu.make_async_remote_copy(
            src_ref=src, dst_ref=dst, send_sem=send_sem.at[kind], recv_sem=recv_sem.at[kind, p],
            device_id=to, device_id_type=MESH,
        )

    def load_kv(p, _):
        for copy in loads(p)[:2]:
            copy.start()
        return 0

    def load_qg(p, _):
        for copy in loads(p)[2:]:
            copy.start()
        return 0

    lax.fori_loop(0, pairs, load_kv, 0)
    lax.fori_loop(0, pairs, load_qg, 0)


    @pl.when(z == 0)
    def _():
        e_in[...] = jnp.zeros_like(e_in)

    @pl.when(z == nz - 1)
    def _():
        te_in[...] = jnp.zeros_like(te_in)

    def to_chip(p, kind, all_ref, in_ref):
        return hop(kind, all_ref.at[1 - c, p], in_ref.at[p], p, sib)

    def z_hop(kind, src, dst, p, half, to):
        rows = pl.ds(half * (HD // 2), HD // 2)
        lane = kind if half == 0 else 8 + kind // 4
        return pltpu.make_async_remote_copy(
            src_ref=src.at[p, rows], dst_ref=dst.at[p, rows],
            send_sem=send_sem.at[lane], recv_sem=recv_sem.at[lane, p],
            device_id=to, device_id_type=MESH,
        )

    def chip_total(p):
        to_chip(p, 0, s_all, x_in).wait_recv()
        c_out[p] = s_all[c, p] + x_in[p]
        hop(1, c_out.at[p], y_in.at[p], p, ypeer).start()

    def along(p):
        hop(1, c_out.at[p], y_in.at[p], p, ypeer).wait_recv()

        for half in range(2):
            rows = slice(half * (HD // 2), (half + 1) * (HD // 2))

            @pl.when(z != 0)
            def _():
                z_hop(2, e_out, e_in, p, half, up).wait_recv()

            @pl.when(z != nz - 1)
            def _():
                e_out[p, rows] = e_in[p, rows] + (c_out[p, rows] + y_in[p, rows])
                z_hop(2, e_out, e_in, p, half, up).start()

        entering = e_in[p]
        other = y_in[p]
        base = entering + jnp.where(y == 1, other, 0.0)
        p_out[p] = base + jnp.where(c == 1, 0.0, s_all[c, p])
        hop(3, p_out.at[p], p_all.at[c, p], p, sib).start()
        p_all[c, p] = base + jnp.where(c == 1, x_in[p], 0.0)

    def column(p):
        to_chip(p, 4, t_all, tx_in).wait_recv()
        for half in range(2):
            rows = slice(half * (HD // 2), (half + 1) * (HD // 2))
            own = t_all[c, p, rows] + tx_in[p, rows]

            @pl.when(z != nz - 1)
            def _():
                z_hop(6, te_out, te_in, p, half, down).wait_recv()

            entering = te_in[p, rows]
            leaving = entering + own
            te_out[p, rows] = leaving

            @pl.when(z != 0)
            def _():
                z_hop(6, te_out, te_in, p, half, down).start()

            tc_out[p, rows] = jnp.where(y == 1, leaving, entering)
        hop(5, tc_out.at[p], ty_in.at[p], p, ypeer).start()

    def across(p):
        hop(5, tc_out.at[p], ty_in.at[p], p, ypeer).wait_recv()
        base = te_in[p] + ty_in[p]
        tp_out[p] = base + jnp.where(c == 0, 0.0, t_all[c, p])
        hop(7, tp_out.at[p], tp_all.at[c, p], p, sib).start()
        tp_all[c, p] = base + jnp.where(c == 0, tx_in[p], 0.0)

    def state(t):
        for copy in loads(t)[:2]:
            copy.wait()
        for j in range(2):
            at = slice(j * HD, (j + 1) * HD)
            s_all[j, t] = tn(kb[t, :, at], vb[t, :, at])

    def prologue(t, _):
        @pl.when(t < pairs)
        def _():
            @pl.when(t >= PEEL)
            def _():
                state(t)
            to_chip(t, 0, s_all, x_in).start()

        @pl.when(t >= LAG_PRO)
        def _():
            chip_total(t - LAG_PRO)

        ahead = t - HEAD_AT

        @pl.when((z == 0) & (ahead >= 0) & (lax.rem(ahead, HEAD_STEP) == 0))
        def _():
            along(ahead // HEAD_STEP)
        return 0

    for t in range(PEEL):
        state(t)
    pl.semaphore_wait(barrier, len(greet))
    lax.fori_loop(0, pairs + LAG_PRO, prologue, 0)

    def forward(p):
        for copy in loads(p)[2:]:
            copy.wait()
        hop(3, p_out.at[p], p_all.at[1 - c, p], p, sib).wait_recv()
        two = range(2)
        at = [slice(j * HD, (j + 1) * HD) for j in two]
        lanes = [pl.ds(pl.multiple_of(p * PW + j * HD, HD), HD) for j in two]
        query = [qb[p, :, at[j]] for j in two]
        key_rows = [kb[p, :, at[j]] for j in two]
        value = [vb[p, :, at[j]] for j in two]
        grad = [gb[p, :, at[j]].astype(F32) for j in two]
        prefix = [p_all[j, p].astype(BF16) for j in two]
        gain = [gain_ref[:, lanes[j]] for j in two]
        scores = [lower(query[j], key_rows[j]) for j in two]
        attended = [by_rows(scores[j], query[j], value[j], prefix[j]) for j in two]
        inverse = [
            lax.rsqrt(jnp.mean(attended[j] * attended[j], axis=-1, keepdims=True) + EPS) for j in two
        ]
        normed = [attended[j] * inverse[j] for j in two]
        product = [grad[j] * normed[j] for j in two]
        mean = [jnp.mean(product[j] * gain[j], axis=-1, keepdims=True) for j in two]
        dattn = [
            (inverse[j] * (grad[j] * gain[j] - normed[j] * mean[j])).astype(BF16) for j in two
        ]
        gstate = [tn(query[j], dattn[j]) for j in two]
        for j in two:
            t_all[j, p] = gstate[j]
        to_chip(p, 4, t_all, tx_in).start()
        for j in two:
            kept[p, :, at[j]] = dattn[j]
            for i, strip in enumerate(scores[j]):
                held[j, p, i * ROWS:(i + 1) * ROWS, :(i + 1) * ROWS] = strip
            gsum[0, :, lanes[j]] = jnp.sum(product[j], axis=0, keepdims=True)
            gb[p, :, at[j]] = (normed[j] * gain[j]).astype(BF16)

    def final(p):
        hop(7, tp_out.at[p], tp_all.at[1 - c, p], p, sib).wait_recv()

        @pl.when(p < pairs - LATE)
        def _():
            gradients(p, qb, kb, vb, kept, held, p_all, tp_all, p, (qb, kb, vb), p)

        @pl.when(p >= pairs - LATE)
        def _():
            late = p - (pairs - LATE)
            for j in range(2):
                prefix_out[j, late] = p_all[j, p]
                suffix_out[j, late] = tp_all[j, p]

    def gain_copy(level, lane, source, to):
        return pltpu.make_async_remote_copy(
            src_ref=gsum.at[level], dst_ref=grecv.at[level, source],
            send_sem=gs_sem.at[level, lane], recv_sem=gr_sem.at[level, source],
            device_id=to, device_id_type=MESH,
        )

    levels = [(near, n_near, gain_near), (z, nz, gain_far), (y, 2, [ypeer])]

    def gain_send(level):
        source, count, others = levels[level]
        grecv[level, source] = gsum[level]
        for lane, other in enumerate(others):
            gain_copy(level, lane, source, other).start()

    def gain_take(level):
        source, count, others = levels[level]
        for r in range(1, count):
            gain_copy(level, 0, lax.rem(source + r, count), others[0]).wait_recv()
        sum_ = grecv[level, 0]
        for r in range(1, count):
            sum_ = sum_ + grecv[level, r]
        gsum[level + 1] = sum_

    def lags(behind):
        column_lag = LAG_COLUMN + LAG_STEP * behind
        across_lag = lax.max(column_lag + LAG_ACROSS, MIN_ACROSS)
        return column_lag, across_lag, lax.max(across_lag + LAG_FIN, MIN_FIN)

    lag_column, lag_across, lag_fin = lags(nz - 1 - z)
    gain_at = lax.max(lag_fin + GAIN_AT, pairs + LAG_FWD)
    most = max(LAG_COLUMN + LAG_STEP * (nz - 1) + LAG_ACROSS, MIN_ACROSS) + LAG_FIN
    most = max(most, MIN_FIN)
    total = max(pairs + most, max(most + GAIN_AT, pairs + LAG_FWD) + 2 * GAIN_STEP + 1)

    head = jnp.where(z == 0, (pairs + LAG_PRO - HEAD_AT + HEAD_STEP - 1) // HEAD_STEP, 0)

    def guarded(p, stage, first=0):
        @pl.when(jnp.logical_and(p >= first, p < pairs))
        def _():
            stage(p)

    def main(t, _):
        guarded(t - LAG_FWD, forward)
        guarded(t - lag_column, column)
        guarded(t - lag_across, across)
        guarded(t, along, head)
        guarded(t - lag_fin, final)

        @pl.when(t == gain_at)
        def _():
            gain_send(0)

        @pl.when(t == gain_at + GAIN_STEP)
        def _():
            gain_take(0)
            gain_send(1)

        @pl.when(t == gain_at + 2 * GAIN_STEP)
        def _():
            gain_take(1)
            gain_send(2)
        return 0

    lax.fori_loop(0, total, main, 0)
    gain_take(2)
    gg_ref[...] = gsum[3]

    for level in range(3):
        source, count, others = levels[level]
        for lane, other in enumerate(others):
            gain_copy(level, lane, source, other).wait_send()
    for kind, all_ref, in_ref, out_ref, y_ref, eo_ref, e_ref, po_ref, pa_ref in (
        (0, s_all, x_in, c_out, y_in, e_out, e_in, p_out, p_all),
        (4, t_all, tx_in, tc_out, ty_in, te_out, te_in, tp_out, tp_all),
    ):
        hop(kind, all_ref.at[1 - c], in_ref, 0, sib).wait_send()
        hop(kind + 1, out_ref, y_ref, 0, ypeer).wait_send()
        reverse = kind == 4

        @pl.when(z != (0 if reverse else nz - 1))
        def _():
            for half in range(2):
                rows = pl.ds(half * (HD // 2), HD // 2)
                pltpu.make_async_remote_copy(
                    src_ref=eo_ref.at[:, rows], dst_ref=e_ref.at[:, rows],
                    send_sem=send_sem.at[(kind + 2) if half == 0 else 8 + kind // 4],
                    recv_sem=recv_sem.at[0, 0],
                    device_id=down if reverse else up, device_id_type=MESH,
                ).wait_send()

        hop(kind + 3, po_ref, pa_ref.at[c], 0, sib).wait_send()


def settle(
    pairs,
    ob, qb, kb, vb, total, kept, held, prefix, suffix,
    o_hbm, gq_hbm, gk_hbm, gv_hbm, result,
    late_q, late_k, late_v, sems,
):
    first = pairs - LATE

    def copies(sources, p, row):
        cols = pl.ds(pl.multiple_of(p * PW, PW), PW)
        return [
            pltpu.make_async_copy(a.at[row], b.at[0, :, cols], sems.at[i, p])
            for i, a, b in sources
        ]

    outs = [(0, ob, o_hbm)]
    grads = [(1, qb, gq_hbm), (2, kb, gk_hbm), (3, vb, gv_hbm)]
    late = [(1, late_q, gq_hbm), (2, late_k, gk_hbm), (3, late_v, gv_hbm)]

    def each(step):
        def early(p, _):
            for copy in copies(outs + grads, p, p):
                step(copy)
            return 0

        def others(p, _):
            for copy in copies(outs, p, p):
                step(copy)
            return 0

        lax.fori_loop(0, first, early, 0)
        lax.fori_loop(first, pairs, others, 0)

    each(lambda copy: copy.start())
    result[...] = total[...]

    def finish(r, _):
        gradients(
            first + r, qb, kb, vb, kept, held, prefix, suffix, r, (late_q, late_k, late_v), r
        )
        for copy in copies(late, first + r, r):
            copy.start()
        return 0

    def drain(r, _):
        for copy in copies(late, first + r, r):
            copy.wait()
        return 0

    lax.fori_loop(0, LATE, finish, 0)
    each(lambda copy: copy.wait())
    lax.fori_loop(0, LATE, drain, 0)


def body(ndp, nctx, queries, keys, values, out_grad, gain):
    _, length, width = queries.shape
    pairs = width // PW
    most = max(2 * ndp, 2, nctx // 4)
    tile = pltpu.VMEM((pairs, length, PW), BF16)
    square = pltpu.VMEM((2, pairs, length, length), BF16)
    one = pltpu.VMEM((pairs, HD, HD), F32)
    two = pltpu.VMEM((2, pairs, HD, HD), F32)
    handed = pltpu.VMEM((2, LATE, HD, HD), F32)
    states = [two, one, one, one, one, one, one, two]
    hbm = pl.BlockSpec(memory_space=pl.ANY)
    vmem = pl.BlockSpec(memory_space=pltpu.VMEM)
    big = jax.ShapeDtypeStruct(queries.shape, BF16)
    out = pl.pallas_call(
        functools.partial(kernel, ndp, nctx, pairs),
        out_shape=(
            tile, tile, tile, tile, pltpu.VMEM((1, width), F32), tile, square, handed, handed,
        ),
        in_specs=[hbm, hbm, hbm, hbm, vmem],
        out_specs=(vmem,) * 9,
        scratch_shapes=[
            *states, *states,
            pltpu.VMEM((4, 1, width), F32),
            pltpu.VMEM((3, most, 1, width), F32),
            pltpu.SemaphoreType.DMA((4, pairs)),
            pltpu.SemaphoreType.DMA((10,)),
            pltpu.SemaphoreType.DMA((10, pairs)),
            pltpu.SemaphoreType.DMA((3, most)),
            pltpu.SemaphoreType.DMA((3, most)),
        ],
        compiler_params=pltpu.CompilerParams(
            collective_id=0, has_side_effects=True, vmem_limit_bytes=30 << 20
        ),
        name="lightning",
    )(queries, keys, values, out_grad, gain.reshape(1, width))
    late = pltpu.VMEM((LATE, length, PW), BF16)
    held = [pltpu.with_memory_space_constraint(a, pltpu.VMEM) for a in out]
    out = pl.pallas_call(
        functools.partial(settle, pairs),
        out_shape=(big, big, big, big, jax.ShapeDtypeStruct((1, width), F32)),
        in_specs=[vmem] * 9,
        out_specs=(hbm, hbm, hbm, hbm, vmem),
        scratch_shapes=[late, late, late, pltpu.SemaphoreType.DMA((4, pairs))],
        compiler_params=pltpu.CompilerParams(vmem_limit_bytes=8 << 20),
        name="settle",
    )(*held)
    return (*out[:4], out[4].reshape(width))


def solution(mesh):
    split = P("dp", "ctx", None)
    return jax.shard_map(
        functools.partial(body, mesh.shape["dp"], mesh.shape["ctx"]),
        mesh=mesh,
        in_specs=(split, split, split, split, P()),
        out_specs=(split, split, split, split, P()),
        check_vma=False,
    )
```
